256 devices in a mesh: tok: 16 (over y, z_lo), wid: 16 (over z_hi, x, core).
Axes of the slice: x: 4, y: 4, z: 8 (z_hi: 2, z_lo: 4; z = z_hi * 4 + z_lo), core: 2. Of those that a mesh axis runs over, the one named last changes fastest.
Arguments:
- g_inverse: bfloat16 [16384, 16384], P('tok', 'wid'), may hold values from -1 to 18, as said below
- a_inverse: bfloat16 [16384, 16384], P('tok', 'wid'), may hold values from -1 to 18, as said below
- query_out: bfloat16 [16384, 128], P(('tok', 'wid')), may hold values from -0.046875 to 0.046875
- query_in: bfloat16 [16384, 128], P(('tok', 'wid')), may hold values from -0.01171875 to 0.01171875
- output_grads: bfloat16 [32768, 16384], P('tok', 'wid'), may hold values from -6 to 6
- activations: bfloat16 [32768, 16384], P('tok', 'wid'), may hold values from -6 to 6
Outputs:
- scores: float32 [8, 32768], P(None, ('tok', 'wid'))
The draws below stay inside these ranges and needn't reach their ends.
Inputs may be any that keep to these rules, and one draw needn't show every extreme that they name: g_inverse is symmetric. a_inverse is symmetric.
All inputs are finite; a program needn't handle non-finite values.
Results may differ from the reference program's by a relative error of at most 0.0041.
Values may be sent and summed in bfloat16 or wider, within the bound.
A program may use at most 64 MiB of HBM per device.

```python
import math
import jax
import jax.numpy as jnp

D = 16384
QUERIES = 8
RANK = 16
TOKENS = 32768


def kron_inverse(key, salt):
    key = jax.random.fold_in(key, salt)
    first, second = jax.random.split(key, 2)
    noise = jax.random.normal(first, (D, D), jnp.float32)
    matrix = (noise + noise.T) * (0.4 / math.sqrt(2.0 * D))
    diag_vals = jax.random.uniform(second, (D,), jnp.float32, 1.0, 2.0)
    matrix = matrix + jnp.diag(diag_vals)
    return matrix


def draw_g_inverse(key, part):
    return kron_inverse(key, 11).astype(jnp.bfloat16)


def draw_a_inverse(key, part):
    return kron_inverse(key, 23).astype(jnp.bfloat16)


def steps_of(key, shape, cuts, least, top_value):
    def one(axis_at, parts):
        steps = jax.random.uniform(jax.random.fold_in(jax.random.fold_in(key, 6), axis_at), (parts,), jnp.float32, least / len(cuts), top_value / len(cuts))
        return jnp.repeat(jnp.exp(steps), shape[axis_at] // parts).reshape((-1,) + (1,) * (len(shape) - axis_at - 1))

    level = one(*cuts[0])
    for cut in cuts[1:]:
        level = level * one(*cut)
    return level


def scatter_about(stream_key, shape, width, most, cuts=(), dtype=jnp.bfloat16):
    array = width * jax.random.normal(stream_key, shape, jnp.float32)
    if cuts:
        array = array * steps_of(stream_key, shape, cuts, -0.22, 0.18)
    return jnp.clip(array, -most, most).astype(dtype)


def setup_inputs(seed: int = 0) -> dict:
    key_of = jax.random.split(jax.random.key(seed), 7)
    return {
        "g_inverse": draw_g_inverse(jax.random.fold_in(key_of[6], 71), 0),
        "a_inverse": draw_a_inverse(jax.random.fold_in(key_of[6], 71), 0),
        "query_out": scatter_about(key_of[2], (D, QUERIES * RANK), D ** -0.5, 0.046875, ((0, 256),)),
        "query_in": scatter_about(key_of[3], (D, QUERIES * RANK), (D * RANK) ** -0.5, 0.01171875, ((0, 256),)),
        "output_grads": scatter_about(key_of[4], (TOKENS, D), 1.0, 6.0, ((0, 16), (1, 16))),
        "activations": scatter_about(key_of[5], (TOKENS, D), 1.0, 6.0, ((0, 16), (1, 16))),
    }


def reference(g_inverse, a_inverse, query_out, query_in, output_grads, activations):
    g_pre = jnp.dot(g_inverse, query_out, preferred_element_type=jnp.float32).astype(jnp.bfloat16)
    a_pre = jnp.dot(a_inverse, query_in, preferred_element_type=jnp.float32).astype(jnp.bfloat16)
    out_proj = jnp.dot(output_grads, g_pre, preferred_element_type=jnp.float32)
    in_proj = jnp.dot(activations, a_pre, preferred_element_type=jnp.float32)
    product = (out_proj * in_proj).reshape(TOKENS, QUERIES, RANK)
    return jnp.sum(product, axis=2).T
```

```python
import jax
import jax.numpy as jnp
from jax import lax
from jax.experimental import pallas as pl
from jax.experimental.pallas import tpu as pltpu
from jax.sharding import PartitionSpec as P

Y, Z, H, X, C = 4, 4, 2, 4, 2
QUERIES = 8
RANK = 16
COLS = QUERIES * RANK
BLOCK = 1024
TOKENS = 2048
PIECE = BLOCK // (H * X * C)
ROWS = COLS // Y
WIDE = BLOCK // Z
SHARE = TOKENS // (H * X * C)


def kernel(
    g_hbm, a_hbm, qo_hbm, qi_hbm, og_hbm, ac_hbm,
    out_ref,
    inv, tok, q, part, yin, zout, zin, pre, own, cout, cin, xout, xin, zhout, zhin,
    load_sem, a_send, a_recv, y_send, y_recv, z_send, z_recv, gz_send, gz_recv,
    gy_send, gy_recv, c_send, c_recv, x_send, x_recv, h_send, h_recv,
):
    my_tok, my_wid = lax.axis_index("tok"), lax.axis_index("wid")
    y, z = my_tok // Z, my_tok % Z
    h, x, c = my_wid // (X * C), (my_wid // C) % X, my_wid % C

    def at(dy=0, dz=0, dh=0, dx=0, dc=0):
        return (
            (y + dy) % Y * Z + (z + dz) % Z,
            (h + dh) % H * (X * C) + (x + dx) % X * C + (c + dc) % C,
        )

    sent = []

    def send(src, dst, send_sem, recv_sem, peer):
        copy = pltpu.make_async_remote_copy(
            src_ref=src, dst_ref=dst, send_sem=send_sem, recv_sem=recv_sem,
            device_id=peer, device_id_type=pl.DeviceIdType.MESH,
        )
        copy.start()
        sent.append(copy)
        return copy

    loads = [
        pltpu.make_async_copy(src, dst, load_sem.at[i])
        for i, (src, dst) in enumerate((
            (qo_hbm, q.at[my_wid, 0]),
            (qi_hbm, q.at[my_wid, 1]),
            (g_hbm, inv.at[0]),
            (a_hbm, inv.at[1]),
            (og_hbm, tok.at[0]),
            (ac_hbm, tok.at[1]),
        ))
    ]
    for load in loads:
        load.start()

    barrier = pltpu.get_barrier_semaphore()
    peers = (
        [at(dh=1), at(dc=1)]
        + [at(dx=d) for d in (1, 2, 3)]
        + [at(dy=d) for d in (1, 2, 3)]
        + [at(dz=d) for d in (1, 2, 3)]
    )
    for peer in peers:
        pl.semaphore_signal(barrier, inc=1, device_id=peer, device_id_type=pl.DeviceIdType.MESH)
    loads[0].wait()
    loads[1].wait()
    pl.semaphore_wait(barrier, len(peers))

    def spread(dh, dx, to_h, to_x, to_c):
        held = q.at[(h - dh) % H * (X * C) + (x - dx) % X * C + c]
        slot = (dh + to_h) * (X * C) + (dx + to_x) * C + to_c
        return send(held, held, a_send.at[slot], a_recv.at[slot], at(dh=to_h, dx=to_x, dc=to_c))

    arrive = {}
    arrive[1, 0, 0] = spread(0, 0, 1, 0, 0)
    for d in (2, 1, 3):
        arrive[0, d, 0] = spread(0, 0, 0, d, 0)
    arrive[0, 0, 1] = spread(0, 0, 0, 0, 1)
    for d in (1, 3, 2):
        arrive[0, d, 0].wait_recv()
        arrive[0, d, 1] = spread(0, d, 0, 0, 1)
    arrive[1, 0, 0].wait_recv()
    for d in (2, 1, 3):
        arrive[1, d, 0] = spread(1, 0, 0, d, 0)
    arrive[1, 0, 1] = spread(1, 0, 0, 0, 1)
    for d in (1, 3, 2):
        arrive[1, d, 0].wait_recv()
        arrive[1, d, 1] = spread(1, d, 0, 0, 1)
    for e in (0, 1):
        for d in range(X):
            arrive[e, d, 1].wait_recv()

    y_copy = {}
    for f in (0, 1):
        loads[2 + f].wait()
        query = q[:, f].reshape(BLOCK, COLS)
        for k in (1, 2, 3, 0):
            wide = pl.ds(pl.multiple_of((z + k) % Z * WIDE, WIDE), WIDE)
            term = lax.dot_general(
                query, inv[f, :, wide], (((0,), (0,)), ((), ())),
                preferred_element_type=jnp.float32,
            )
            part[f, k] = term.reshape(Y, ROWS, WIDE)
            for d in (2, 1, 3):
                y_copy[f, k, d] = send(
                    part.at[f, k, (y + d) % Y], yin.at[f, k, d - 1],
                    y_send.at[f, k, d - 1], y_recv.at[f, k, d - 1], at(dy=d),
                )

    z_copy = {}
    mine = {}
    for f in (0, 1):
        for k in (1, 2, 3, 0):
            for d in (1, 3, 2):
                y_copy[f, k, d].wait_recv()
            total = part[f, k, y] + ((yin[f, k, 0] + yin[f, k, 1]) + yin[f, k, 2])
            zout[f, k] = total
            if k:
                z_copy[f, k] = send(
                    zout.at[f, k], zin.at[f, k - 1],
                    z_send.at[f, k - 1], z_recv.at[f, k - 1], at(dz=k),
                )

    gz_copy, gy_copy = {}, {}

    def along_y(f, k):
        held = pre.at[f, (z - k) % Z, y]
        for d in (2, 1, 3):
            gy_copy[f, k, d] = send(
                held, held, gy_send.at[f, k, d - 1], gy_recv.at[f, k, d - 1], at(dy=d)
            )

    for f in (0, 1):
        for k in (1, 2, 3):
            z_copy[f, k].wait_recv()
        total = zout[f, 0] + ((zin[f, 0] + zin[f, 1]) + zin[f, 2])
        pre[f, z, y] = total.astype(jnp.bfloat16)
        held = pre.at[f, z, y]
        for k in (1, 2, 3):
            gz_copy[f, k] = send(
                held, held, gz_send.at[f, k - 1], gz_recv.at[f, k - 1], at(dz=k)
            )
        along_y(f, 0)
    for f in (0, 1):
        for k in (1, 2, 3):
            gz_copy[f, k].wait_recv()
            along_y(f, k)

    c_copy = {}
    for f in (0, 1):
        for k in range(Z):
            for d in (1, 3, 2):
                gy_copy[f, k, d].wait_recv()
        loads[4 + f].wait()
        for e in (1, 0):
            to = (h + e) % H
            for i in range(X):
                rows = pl.ds(pl.multiple_of((to * X + i) * (C * SHARE), C * SHARE), C * SHARE)
                proj = None
                for k in range(Z):
                    term = lax.dot_general(
                        pre[f, k].reshape(COLS, WIDE),
                        tok[f, rows, k * WIDE:(k + 1) * WIDE],
                        (((1,), (1,)), ((), ())),
                        preferred_element_type=jnp.float32,
                    )
                    proj = term if proj is None else proj + term
                low, high = proj[:, :SHARE], proj[:, SHARE:]
                first = c == 0
                own[f, e, i] = jnp.where(first, low, high)
                cout[f, e, i] = jnp.where(first, high, low).astype(jnp.bfloat16)
            c_copy[f, e] = send(
                cout.at[f, e], cin.at[f, e], c_send.at[f, e], c_recv.at[f, e], at(dc=1)
            )

    x_copy = {}
    for f in (0, 1):
        for e in (1, 0):
            c_copy[f, e].wait_recv()
            for d in (2, 1, 3):
                i = (x + d) % X
                xout[f, e, d - 1] = (own[f, e, i] + cin[f, e, i].astype(jnp.float32)).astype(jnp.bfloat16)
                x_copy[f, e, d] = send(
                    xout.at[f, e, d - 1], xin.at[f, e, d - 1],
                    x_send.at[f, e, d - 1], x_recv.at[f, e, d - 1], at(dx=d),
                )

    def over_x(f, e):
        for d in (1, 3, 2):
            x_copy[f, e, d].wait_recv()
        total = own[f, e, x] + cin[f, e, x].astype(jnp.float32)
        for d in (1, 2, 3):
            total = total + xin[f, e, d - 1].astype(jnp.float32)
        return total

    h_copy = {}
    for f in (0, 1):
        zhout[f] = over_x(f, 1).astype(jnp.bfloat16)
        h_copy[f] = send(zhout.at[f], zhin.at[f], h_send.at[f], h_recv.at[f], at(dh=1))
    proj = [over_x(f, 0) for f in (0, 1)]
    for f in (0, 1):
        h_copy[f].wait_recv()
        proj[f] = proj[f] + zhin[f].astype(jnp.float32)
    out_ref[...] = jnp.sum((proj[0] * proj[1]).reshape(QUERIES, RANK, SHARE), axis=1)
    for copy in sent:
        copy.wait_send()


def shards(*args):
    bf16, f32 = jnp.bfloat16, jnp.float32
    dma = pltpu.SemaphoreType.DMA
    pairs = lambda *shape: [dma(shape), dma(shape)]
    return pl.pallas_call(
        kernel,
        out_shape=jax.ShapeDtypeStruct((QUERIES, SHARE), f32),
        in_specs=[pl.BlockSpec(memory_space=pl.ANY)] * 6,
        out_specs=pl.BlockSpec(memory_space=pltpu.VMEM),
        scratch_shapes=[
            pltpu.VMEM((2, BLOCK, BLOCK), bf16),
            pltpu.VMEM((2, TOKENS, BLOCK), bf16),
            pltpu.VMEM((H * X * C, 2, PIECE, COLS), bf16),
            pltpu.VMEM((2, Z, Y, ROWS, WIDE), f32),
            pltpu.VMEM((2, Z, Y - 1, ROWS, WIDE), f32),
            pltpu.VMEM((2, Z, ROWS, WIDE), f32),
            pltpu.VMEM((2, Z - 1, ROWS, WIDE), f32),
            pltpu.VMEM((2, Z, Y, ROWS, WIDE), bf16),
            pltpu.VMEM((2, H, X, COLS, SHARE), f32),
            pltpu.VMEM((2, H, X, COLS, SHARE), bf16),
            pltpu.VMEM((2, H, X, COLS, SHARE), bf16),
            pltpu.VMEM((2, H, X - 1, COLS, SHARE), bf16),
            pltpu.VMEM((2, H, X - 1, COLS, SHARE), bf16),
            pltpu.VMEM((2, COLS, SHARE), bf16),
            pltpu.VMEM((2, COLS, SHARE), bf16),
            dma((6,)),
            *pairs(H * X * C),
            *pairs(2, Z, Y - 1),
            *pairs(2, Z - 1),
            *pairs(2, Z - 1),
            *pairs(2, Z, Y - 1),
            *pairs(2, H),
            *pairs(2, H, X - 1),
            *pairs(2),
        ],
        compiler_params=pltpu.CompilerParams(
            collective_id=0, has_side_effects=True, vmem_limit_bytes=60 << 20
        ),
    )(*args)


def solution(mesh):
    return jax.shard_map(
        shards,
        mesh=mesh,
        in_specs=(
            P("tok", "wid"),
            P("tok", "wid"),
            P(("tok", "wid"), None),
            P(("tok", "wid"), None),
            P("tok", "wid"),
            P("tok", "wid"),
        ),
        out_specs=P(None, ("tok", "wid")),
        check_vma=False,
    )
```

```python
import jax
import jax.numpy as jnp
from jax import lax
from jax.experimental import pallas as pl
from jax.experimental.pallas import tpu as pltpu
from jax.sharding import PartitionSpec as P

Y, Z, H, X, C = 4, 4, 2, 4, 2
QUERIES = 8
RANK = 16
COLS = QUERIES * RANK
BLOCK = 1024
TOKENS = 2048
PIECE = BLOCK // (H * X * C)
ROWS = COLS // Y // 2
WIDE = BLOCK // Z
SHARE = TOKENS // (H * X * C)


def kernel(
    g_hbm, a_hbm, qo_hbm, qi_hbm, og_hbm, ac_hbm,
    out_ref,
    inv, tok, q, part, yin, yout, zout, zin, pre, own, cout, cin, xout, xin, zhout, zhin,
    load_sem, a_send, a_recv, y_send, y_recv, z_send, z_recv, gz_send, gz_recv,
    gy_send, gy_recv, c_send, c_recv, x_send, x_recv, h_send, h_recv,
):
    my_tok, my_wid = lax.axis_index("tok"), lax.axis_index("wid")
    y, z = my_tok // Z, my_tok % Z
    h, x, c = my_wid // (X * C), (my_wid // C) % X, my_wid % C

    def at(dy=0, dz=0, dh=0, dx=0, dc=0):
        return (
            (y + dy) % Y * Z + (z + dz) % Z,
            (h + dh) % H * (X * C) + (x + dx) % X * C + (c + dc) % C,
        )

    sent = []

    def send(src, dst, send_sem, recv_sem, peer):
        copy = pltpu.make_async_remote_copy(
            src_ref=src, dst_ref=dst, send_sem=send_sem, recv_sem=recv_sem,
            device_id=peer, device_id_type=pl.DeviceIdType.MESH,
        )
        copy.start()
        sent.append(copy)
        return copy

    loads = [
        pltpu.make_async_copy(src, dst, load_sem.at[i])
        for i, (src, dst) in enumerate((
            (qo_hbm, q.at[0, my_wid]),
            (qi_hbm, q.at[1, my_wid]),
            (g_hbm, inv.at[0]),
            (a_hbm, inv.at[1]),
            (og_hbm, tok.at[0]),
            (ac_hbm, tok.at[1]),
        ))
    ]
    for load in loads:
        load.start()

    barrier = pltpu.get_barrier_semaphore()
    peers = (
        [at(dh=1), at(dc=1)]
        + [at(dx=d, dc=e) for d in (1, 2, 3) for e in (0, 1)]
        + [at(dy=d) for d in (1, 3)]
        + [at(dy=2)]
        + [at(dz=d) for d in (1, 2, 3)]
    )
    for peer in peers:
        pl.semaphore_signal(barrier, inc=1, device_id=peer, device_id_type=pl.DeviceIdType.MESH)
    pl.semaphore_wait(barrier, len(peers))

    a_copy = {}

    def spread(f, src, dh, to_h, to_x, to_c):
        slot = (dh + to_h) * (X * C) + to_x * C + to_c
        a_copy[f, slot] = send(
            src, q.at[f, (h - dh) % H * (X * C) + x * C + c],
            a_send.at[f, slot], a_recv.at[f, slot], at(dh=to_h, dx=to_x, dc=to_c),
        )

    around = [(d, e) for d in (2, 1, 3) for e in (0, 1)] + [(0, 1)]
    mine = (qo_hbm, qi_hbm)
    for f in (0, 1):
        spread(f, mine[f], 0, 1, 0, 0)
    for f in (0, 1):
        for d, e in around:
            spread(f, mine[f], 0, 0, d, e)
    for f in (0, 1):
        a_copy[f, X * C].wait_recv()
        for d, e in around:
            spread(f, q.at[f, (h + 1) % H * (X * C) + x * C + c], 1, 0, d, e)

    r_copy, d_copy, s_copy, z_copy, gz_copy, gy_copy = {}, {}, {}, {}, {}, {}
    ORDER = (1, 2, 3, 0)

    def way(s):
        return 1 if s % 2 == 0 else -1

    def factor_terms(s):
        f, r = s // 2, s % 2
        if r == 0:
            loads[f].wait()
            loads[2 + f].wait()
            for slot in range(1, H * X * C):
                if slot != X * C:
                    a_copy[f, slot].wait_recv()
            query = q[f].reshape(BLOCK, COLS)
        for k in ORDER:
            if r == 0:
                wide = pl.ds(pl.multiple_of((z + k) % Z * WIDE, WIDE), WIDE)
                term = lax.dot_general(
                    query, inv[f, :, wide], (((0,), (0,)), ((), ())),
                    preferred_element_type=jnp.float32,
                ).reshape(Y, 2, ROWS, WIDE)
                part[2 * f, k] = term[:, 0]
                part[2 * f + 1, k] = term[:, 1]
            r_copy[s, k] = send(
                part.at[s, k, (y + 2) % Y], yin.at[s, k, 0],
                y_send.at[s, k, 0], y_recv.at[s, k, 0], at(dy=way(s)),
            )
            d_copy[s, k] = send(
                part.at[s, k, (y - way(s)) % Y], yin.at[s, k, 1],
                y_send.at[s, k, 1], y_recv.at[s, k, 1], at(dy=-way(s)),
            )

    def relay(s):
        for k in ORDER:
            r_copy[s, k].wait_recv()
            yout[s, k] = part[s, k, (y + way(s)) % Y] + yin[s, k, 0]
            s_copy[s, k] = send(
                yout.at[s, k], yin.at[s, k, 2],
                y_send.at[s, k, 2], y_recv.at[s, k, 2], at(dy=way(s)),
            )

    def over_y(s):
        for k in ORDER:
            d_copy[s, k].wait_recv()
            s_copy[s, k].wait_recv()
            zout[s, k] = part[s, k, y] + (yin[s, k, 1] + yin[s, k, 2])
            if k:
                z_copy[s, k] = send(
                    zout.at[s, k], zin.at[s, k - 1],
                    z_send.at[s, k - 1], z_recv.at[s, k - 1], at(dz=k),
                )

    def along_y(s, k):
        held = pre.at[s // 2, (z - k) % Z, y, s % 2]
        for d in (2, 1, 3):
            gy_copy[s, k, d] = send(
                held, held, gy_send.at[s, k, d - 1], gy_recv.at[s, k, d - 1], at(dy=d)
            )

    def over_z(s):
        for k in (1, 2, 3):
            z_copy[s, k].wait_recv()
        total = zout[s, 0] + ((zin[s, 0] + zin[s, 1]) + zin[s, 2])
        pre[s // 2, z, y, s % 2] = total.astype(jnp.bfloat16)
        held = pre.at[s // 2, z, y, s % 2]
        for k in (1, 2, 3):
            gz_copy[s, k] = send(
                held, held, gz_send.at[s, k - 1], gz_recv.at[s, k - 1], at(dz=k)
            )
        along_y(s, 0)

    def onward(s):
        for k in (1, 2, 3):
            gz_copy[s, k].wait_recv()
            along_y(s, k)

    factor_terms(0)
    factor_terms(1)
    factor_terms(2)
    relay(0)
    factor_terms(3)
    relay(1)
    over_y(0)
    relay(2)
    over_y(1)
    over_z(0)
    relay(3)
    over_y(2)
    over_z(1)
    onward(0)
    over_y(3)
    over_z(2)
    onward(1)
    over_z(3)
    onward(2)
    onward(3)

    c_copy = {}
    for f in (0, 1):
        for s in (2 * f, 2 * f + 1):
            for k in range(Z):
                for d in (1, 3, 2):
                    gy_copy[s, k, d].wait_recv()
        loads[4 + f].wait()
        for e in (1, 0):
            to = (h + e) % H
            for i in range(X):
                rows = pl.ds(pl.multiple_of((to * X + i) * (C * SHARE), C * SHARE), C * SHARE)
                proj = None
                for k in range(Z):
                    term = lax.dot_general(
                        pre[f, k].reshape(COLS, WIDE),
                        tok[f, rows, k * WIDE:(k + 1) * WIDE],
                        (((1,), (1,)), ((), ())),
                        preferred_element_type=jnp.float32,
                    )
                    proj = term if proj is None else proj + term
                low, high = proj[:, :SHARE], proj[:, SHARE:]
                first = c == 0
                own[f, e, i] = jnp.where(first, low, high)
                cout[f, e, i] = jnp.where(first, high, low).astype(jnp.bfloat16)
            c_copy[f, e] = send(
                cout.at[f, e], cin.at[f, e], c_send.at[f, e], c_recv.at[f, e], at(dc=1)
            )

    x_copy = {}
    for f in (0, 1):
        for e in (1, 0):
            c_copy[f, e].wait_recv()
            for d in (2, 1, 3):
                i = (x + d) % X
                xout[f, e, d - 1] = (own[f, e, i] + cin[f, e, i].astype(jnp.float32)).astype(jnp.bfloat16)
                x_copy[f, e, d] = send(
                    xout.at[f, e, d - 1], xin.at[f, e, d - 1],
                    x_send.at[f, e, d - 1], x_recv.at[f, e, d - 1], at(dx=d),
                )

    def over_x(f, e):
        for d in (1, 3, 2):
            x_copy[f, e, d].wait_recv()
        total = own[f, e, x] + cin[f, e, x].astype(jnp.float32)
        for d in (1, 2, 3):
            total = total + xin[f, e, d - 1].astype(jnp.float32)
        return total

    h_copy = {}
    for f in (0, 1):
        zhout[f] = over_x(f, 1).astype(jnp.bfloat16)
        h_copy[f] = send(zhout.at[f], zhin.at[f], h_send.at[f], h_recv.at[f], at(dh=1))
    proj = [over_x(f, 0) for f in (0, 1)]
    for f in (0, 1):
        h_copy[f].wait_recv()
        proj[f] = proj[f] + zhin[f].astype(jnp.float32)
    out_ref[...] = jnp.sum((proj[0] * proj[1]).reshape(QUERIES, RANK, SHARE), axis=1)
    for copy in sent:
        copy.wait_send()


def shards(*args):
    bf16, f32 = jnp.bfloat16, jnp.float32
    dma = pltpu.SemaphoreType.DMA
    pairs = lambda *shape: [dma(shape), dma(shape)]
    return pl.pallas_call(
        kernel,
        out_shape=jax.ShapeDtypeStruct((QUERIES, SHARE), f32),
        in_specs=[pl.BlockSpec(memory_space=pl.ANY)] * 6,
        out_specs=pl.BlockSpec(memory_space=pltpu.VMEM),
        scratch_shapes=[
            pltpu.VMEM((2, BLOCK, BLOCK), bf16),
            pltpu.VMEM((2, TOKENS, BLOCK), bf16),
            pltpu.VMEM((2, H * X * C, PIECE, COLS), bf16),
            pltpu.VMEM((4, Z, Y, ROWS, WIDE), f32),
            pltpu.VMEM((4, Z, 3, ROWS, WIDE), f32),
            pltpu.VMEM((4, Z, ROWS, WIDE), f32),
            pltpu.VMEM((4, Z, ROWS, WIDE), f32),
            pltpu.VMEM((4, Z - 1, ROWS, WIDE), f32),
            pltpu.VMEM((2, Z, Y, 2, ROWS, WIDE), bf16),
            pltpu.VMEM((2, H, X, COLS, SHARE), f32),
            pltpu.VMEM((2, H, X, COLS, SHARE), bf16),
            pltpu.VMEM((2, H, X, COLS, SHARE), bf16),
            pltpu.VMEM((2, H, X - 1, COLS, SHARE), bf16),
            pltpu.VMEM((2, H, X - 1, COLS, SHARE), bf16),
            pltpu.VMEM((2, COLS, SHARE), bf16),
            pltpu.VMEM((2, COLS, SHARE), bf16),
            dma((6,)),
            *pairs(2, H * X * C),
            *pairs(4, Z, 3),
            *pairs(4, Z - 1),
            *pairs(4, Z - 1),
            *pairs(4, Z, Y - 1),
            *pairs(2, H),
            *pairs(2, H, X - 1),
            *pairs(2),
        ],
        compiler_params=pltpu.CompilerParams(
            collective_id=0, has_side_effects=True, vmem_limit_bytes=60 << 20
        ),
    )(*args)


def solution(mesh):
    return jax.shard_map(
        shards,
        mesh=mesh,
        in_specs=(
            P("tok", "wid"),
            P("tok", "wid"),
            P(("tok", "wid"), None),
            P(("tok", "wid"), None),
            P("tok", "wid"),
            P("tok", "wid"),
        ),
        out_specs=P(None, ("tok", "wid")),
        check_vma=False,
    )
```

```python
import jax
import jax.numpy as jnp
from jax import lax
from jax.experimental import pallas as pl
from jax.experimental.pallas import tpu as pltpu
from jax.sharding import PartitionSpec as P

Y, Z, H, X, C = 4, 4, 2, 4, 2
QUERIES = 8
RANK = 16
COLS = QUERIES * RANK
BLOCK = 1024
TOKENS = 2048
PIECE = BLOCK // (H * X * C)
ROWS = COLS // Y
WIDE = BLOCK // Z
SHARE = TOKENS // (H * X * C)


def kernel(
    g_hbm, a_hbm, qo_hbm, qi_hbm, og_hbm, ac_hbm,
    out_ref,
    inv, tok, q, part, yin, zout, zin, pre, own, cout, cin, xout, xin, zhout, zhin,
    load_sem, a_send, a_recv, y_send, y_recv, z_send, z_recv, gz_send, gz_recv,
    gy_send, gy_recv, c_send, c_recv, x_send, x_recv, h_send, h_recv,
):
    f32, bf16 = jnp.float32, jnp.bfloat16
    my_tok, my_wid = lax.axis_index("tok"), lax.axis_index("wid")
    y, z = my_tok // Z, my_tok % Z
    h, x, c = my_wid // (X * C), (my_wid // C) % X, my_wid % C

    def at(dy=0, dz=0, dh=0, dx=0, dc=0):
        return (
            (y + dy) % Y * Z + (z + dz) % Z,
            (h + dh) % H * (X * C) + (x + dx) % X * C + (c + dc) % C,
        )

    def copy(src, dst, send_sem, recv_sem, peer):
        return pltpu.make_async_remote_copy(
            src_ref=src, dst_ref=dst, send_sem=send_sem, recv_sem=recv_sem,
            device_id=peer, device_id_type=pl.DeviceIdType.MESH,
        )

    def send(src, dst, send_sem, recv_sem, peer):
        copy(src, dst, send_sem, recv_sem, peer).start()

    def wait_recv(ref, sem):
        copy(ref, ref, load_sem.at[0], sem, at(dc=1)).wait_recv()

    def wait_send(ref, sem):
        copy(ref, ref, sem, load_sem.at[0], at(dc=1)).wait_send()

    loads = [
        pltpu.make_async_copy(src, dst, load_sem.at[i])
        for i, (src, dst) in enumerate((
            (qo_hbm, q.at[my_wid, 0]),
            (qi_hbm, q.at[my_wid, 1]),
            (g_hbm, inv.at[0]),
            (a_hbm, inv.at[1]),
            (og_hbm, tok.at[0]),
            (ac_hbm, tok.at[1]),
        ))
    ]
    for load in loads:
        load.start()

    around = [(d, e) for d in (2, 1, 3) for e in (0, 1)] + [(0, 1)]
    barrier = pltpu.get_barrier_semaphore()
    peers = (
        [at(dh=1)]
        + [at(dx=d, dc=e) for d, e in around]
        + [at(dy=d) for d in (2, 1, 3)]
        + [at(dz=d) for d in (1, 2, 3)]
    )
    for peer in peers:
        pl.semaphore_signal(barrier, inc=1, device_id=peer, device_id_type=pl.DeviceIdType.MESH)
    pl.semaphore_wait(barrier, len(peers))

    far = q.at[(my_wid + X * C) % (H * X * C)]
    mine = q.at[my_wid]
    for f, src in enumerate((qo_hbm, qi_hbm)):
        send(src, mine.at[f], a_send, a_recv.at[0], at(dh=1))
    loads[0].wait()
    loads[1].wait()
    for d, e in around:
        send(mine, mine, a_send, a_recv.at[1], at(dx=d, dc=e))
    wait_recv(far, a_recv.at[0])
    for d, e in around:
        send(far, far, a_send, a_recv.at[1], at(dx=d, dc=e))
    wait_recv(q.at[pl.ds(0, 2 * len(around))], a_recv.at[1])

    ORDER = (1, 2, 3, 0)
    for f in (0, 1):
        loads[2 + f].wait()
        query = q[:, f].reshape(BLOCK, COLS)
        for k in ORDER:
            wide = pl.ds(pl.multiple_of((z + k) % Z * WIDE, WIDE), WIDE)
            term = lax.dot_general(
                query, inv[f, :, wide], (((0,), (0,)), ((), ())), preferred_element_type=f32
            )
            part[f, k] = term.reshape(Y, ROWS, WIDE)
            for d in (2, 1, 3):
                send(
                    part.at[f, k, (y + d) % Y], yin.at[f, k, d - 1],
                    y_send, y_recv.at[f, k], at(dy=d),
                )

    def over_y(f, k):
        wait_recv(yin.at[f, k], y_recv.at[f, k])
        zout[f, k] = part[f, k, y] + ((yin[f, k, 0] + yin[f, k, 1]) + yin[f, k, 2])
        if k:
            send(zout.at[f, k], zin.at[f, k - 1], z_send, z_recv.at[f], at(dz=k))

    def along_y(f, k):
        held = pre.at[f, (z - k) % Z, y]
        for d in (2, 1, 3):
            send(held, held, gy_send.at[f], gy_recv.at[f], at(dy=d))

    def over_z(f):
        wait_recv(zin.at[f], z_recv.at[f])
        total = zout[f, 0] + ((zin[f, 0] + zin[f, 1]) + zin[f, 2])
        pre[f, z, y] = total.astype(bf16)
        held = pre.at[f, z, y]
        for k in (3, 2, 1):
            send(held, held, gz_send.at[f], gz_recv.at[f, k - 1], at(dz=k))
        along_y(f, 0)

    def onward(f):
        for k in (1, 2, 3):
            wait_recv(pre.at[f, 0, 0], gz_recv.at[f, k - 1])
            along_y(f, k)

    def project(f):
        wait_recv(pre.at[f, pl.ds(0, Y - 1)], gy_recv.at[f])
        loads[4 + f].wait()
        first = c == 0
        for e in (1, 0):
            to = (h + e) % H
            for i in range(X):
                rows = pl.ds(pl.multiple_of((to * X + i) * (C * SHARE), C * SHARE), C * SHARE)
                proj = None
                for k in range(Z):
                    term = lax.dot_general(
                        pre[f, k].reshape(COLS, WIDE),
                        tok[f, rows, k * WIDE:(k + 1) * WIDE],
                        (((1,), (1,)), ((), ())),
                        preferred_element_type=f32,
                    )
                    proj = term if proj is None else proj + term
                low, high = proj[:, :SHARE], proj[:, SHARE:]
                own[f, e, i] = jnp.where(first, low, high)
                cout[f, e, i] = jnp.where(first, high, low).astype(bf16)
            send(cout.at[f, e], cin.at[f, e], c_send, c_recv.at[f, e], at(dc=1))

    def along_x(f, e):
        wait_recv(cin.at[f, e], c_recv.at[f, e])
        for d in (2, 1, 3):
            i = (x + d) % X
            xout[f, e, d - 1] = (own[f, e, i] + cin[f, e, i].astype(f32)).astype(bf16)
            send(
                xout.at[f, e, d - 1], xin.at[f, e, d - 1],
                x_send, x_recv.at[f, e], at(dx=d),
            )

    def over_x(f, e):
        total = own[f, e, x] + cin[f, e, x].astype(f32)
        wait_recv(xin.at[f, e], x_recv.at[f, e])
        for d in (1, 2, 3):
            total = total + xin[f, e, d - 1].astype(f32)
        return total

    def along_h(f):
        zhout[f] = over_x(f, 1).astype(bf16)
        send(zhout.at[f], zhin.at[f], h_send, h_recv.at[f], at(dh=1))

    for k in ORDER:
        over_y(0, k)
    over_z(0)
    for k in ORDER[:3]:
        over_y(1, k)
    onward(0)
    over_y(1, 0)
    over_z(1)
    project(0)
    onward(1)
    along_x(0, 1)
    along_x(0, 0)
    wait_send(q.at[pl.ds(0, 2 * len(around) + 1)], a_send)
    wait_send(yin, y_send)
    wait_send(zin, z_send)
    project(1)
    along_h(0)
    along_x(1, 1)
    along_x(1, 0)
    wait_send(pre.at[0, pl.ds(0, Y - 1)], gy_send.at[0])
    wait_send(pre.at[1, pl.ds(0, Y - 1)], gy_send.at[1])
    for f in (0, 1):
        wait_send(pre.at[f, 0, pl.ds(0, Z - 1)], gz_send.at[f])
    along_h(1)
    wait_send(cout, c_send)
    proj = [over_x(f, 0) for f in (0, 1)]
    wait_send(xout, x_send)
    wait_send(zhout, h_send)
    for f in (0, 1):
        wait_recv(zhin.at[f], h_recv.at[f])
        proj[f] = proj[f] + zhin[f].astype(f32)
    out_ref[...] = jnp.sum((proj[0] * proj[1]).reshape(QUERIES, RANK, SHARE), axis=1)


def shards(*args):
    bf16, f32 = jnp.bfloat16, jnp.float32
    dma = pltpu.SemaphoreType.DMA
    return pl.pallas_call(
        kernel,
        out_shape=jax.ShapeDtypeStruct((QUERIES, SHARE), f32),
        in_specs=[pl.BlockSpec(memory_space=pl.ANY)] * 6,
        out_specs=pl.BlockSpec(memory_space=pltpu.VMEM),
        scratch_shapes=[
            pltpu.VMEM((2, BLOCK, BLOCK), bf16),
            pltpu.VMEM((2, TOKENS, BLOCK), bf16),
            pltpu.VMEM((H * X * C, 2, PIECE, COLS), bf16),
            pltpu.VMEM((2, Z, Y, ROWS, WIDE), f32),
            pltpu.VMEM((2, Z, Y - 1, ROWS, WIDE), f32),
            pltpu.VMEM((2, Z, ROWS, WIDE), f32),
            pltpu.VMEM((2, Z - 1, ROWS, WIDE), f32),
            pltpu.VMEM((2, Z, Y, ROWS, WIDE), bf16),
            pltpu.VMEM((2, H, X, COLS, SHARE), f32),
            pltpu.VMEM((2, H, X, COLS, SHARE), bf16),
            pltpu.VMEM((2, H, X, COLS, SHARE), bf16),
            pltpu.VMEM((2, H, X - 1, COLS, SHARE), bf16),
            pltpu.VMEM((2, H, X - 1, COLS, SHARE), bf16),
            pltpu.VMEM((2, COLS, SHARE), bf16),
            pltpu.VMEM((2, COLS, SHARE), bf16),
            dma((6,)),
            dma, dma((2,)),
            dma, dma((2, Z)),
            dma, dma((2,)),
            dma((2,)), dma((2, Z - 1)),
            dma((2,)), dma((2,)),
            dma, dma((2, H)),
            dma, dma((2, H)),
            dma, dma((2,)),
        ],
        compiler_params=pltpu.CompilerParams(
            collective_id=0, has_side_effects=True, vmem_limit_bytes=60 << 20
        ),
    )(*args)


def solution(mesh):
    return jax.shard_map(
        shards,
        mesh=mesh,
        in_specs=(
            P("tok", "wid"),
            P("tok", "wid"),
            P(("tok", "wid"), None),
            P(("tok", "wid"), None),
            P("tok", "wid"),
            P("tok", "wid"),
        ),
        out_specs=P(None, ("tok", "wid")),
        check_vma=False,
    )
```

```python
import jax
import jax.numpy as jnp
from jax import lax
from jax.experimental import pallas as pl
from jax.experimental.pallas import tpu as pltpu
from jax.sharding import PartitionSpec as P

Y, Z, H, X, C = 4, 4, 2, 4, 2
QUERIES = 8
RANK = 16
COLS = QUERIES * RANK
BLOCK = 1024
TOKENS = 2048
PIECE = BLOCK // (H * X * C)
ROWS = COLS // Y // 2
WIDE = BLOCK // Z
SHARE = TOKENS // (H * X * C)


def kernel(
    g_hbm, a_hbm, qo_hbm, qi_hbm, og_hbm, ac_hbm,
    out_ref,
    inv, tok, q, part, yin, zout, zin, pre, own, cout, cin, xout, xin, zhout, zhin,
    load_sem, a_send, a_recv, y_send, y_recv, z_send, z_recv, gz_send, gz_recv,
    gy_send, gy_recv, c_send, c_recv, x_send, x_recv, h_send, h_recv,
):
    f32, bf16 = jnp.float32, jnp.bfloat16
    my_tok, my_wid = lax.axis_index("tok"), lax.axis_index("wid")
    y, z = my_tok // Z, my_tok % Z
    h, x, c = my_wid // (X * C), (my_wid // C) % X, my_wid % C

    other_z = (z, z + 1 - 2 * (z % 2), (z + 2) % Z, Z - 1 - z)

    def at(dy=0, dz=0, dh=0, dx=0, dc=0):
        return (
            (y + dy) % Y * Z + other_z[dz],
            (h + dh) % H * (X * C) + (x + dx) % X * C + (c + dc) % C,
        )

    def copy(src, dst, send_sem, recv_sem, peer):
        return pltpu.make_async_remote_copy(
            src_ref=src, dst_ref=dst, send_sem=send_sem, recv_sem=recv_sem,
            device_id=peer, device_id_type=pl.DeviceIdType.MESH,
        )

    def send(src, dst, send_sem, recv_sem, peer):
        copy(src, dst, send_sem, recv_sem, peer).start()

    def wait_recv(ref, sem):
        copy(ref, ref, load_sem.at[0], sem, at(dc=1)).wait_recv()

    def wait_send(ref, sem):
        copy(ref, ref, sem, load_sem.at[0], at(dc=1)).wait_send()

    loads = [
        pltpu.make_async_copy(src, dst, load_sem.at[i])
        for i, (src, dst) in enumerate((
            (qo_hbm, q.at[0, my_wid]),
            (qi_hbm, q.at[1, my_wid]),
            (g_hbm, inv.at[0]),
            (a_hbm, inv.at[1]),
            (og_hbm, tok.at[0]),
            (ac_hbm, tok.at[1]),
        ))
    ]
    for load in loads:
        load.start()

    around = [(d, e) for d in (2, 1, 3) for e in (0, 1)] + [(0, 1)]
    barrier = pltpu.get_barrier_semaphore()
    peers = (
        [at(dh=1)]
        + [at(dx=d, dc=e) for d, e in around]
        + [at(dy=d) for d in (2, 1, 3)]
        + [at(dz=d) for d in (1, 2, 3)]
    )
    for peer in peers:
        pl.semaphore_signal(barrier, inc=1, device_id=peer, device_id_type=pl.DeviceIdType.MESH)
    pl.semaphore_wait(barrier, len(peers))

    far = (my_wid + X * C) % (H * X * C)
    for f, src in enumerate((qo_hbm, qi_hbm)):
        send(src, q.at[f, my_wid], a_send, a_recv.at[f, 0], at(dh=1))
    for f, src in enumerate((qo_hbm, qi_hbm)):
        for d, e in around:
            send(src, q.at[f, my_wid], a_send, a_recv.at[f, 1], at(dx=d, dc=e))
    for f in (0, 1):
        wait_recv(q.at[f, far], a_recv.at[f, 0])
        for d, e in around:
            send(q.at[f, far], q.at[f, far], a_send, a_recv.at[f, 1], at(dx=d, dc=e))

    ORDER = (3, 2, 1, 0)

    def terms(f, first):
        loads[f].wait()
        loads[2 + f].wait()
        wait_recv(q.at[f, pl.ds(0, 2 * len(around))], a_recv.at[f, 1])
        query = q[f].reshape(BLOCK, COLS)
        for k in ORDER:
            wide = pl.ds(pl.multiple_of(other_z[k] * WIDE, WIDE), WIDE)
            term = lax.dot_general(
                query, inv[f, :, wide], (((0,), (0,)), ((), ())), preferred_element_type=f32
            ).reshape(Y, 2, ROWS, WIDE)
            part[2 * f, k] = term[:, 0]
            part[2 * f + 1, k] = term[:, 1]
            for s in first:
                share_out(s, k)

    def share_out(s, k):
        for d in (2, 1, 3):
            send(
                part.at[s, k, (y + d) % Y], yin.at[s, k, d - 1],
                y_send, y_recv.at[s, k], at(dy=d),
            )

    def share(s):
        for k in ORDER:
            share_out(s, k)

    def over_y(s):
        for k in ORDER:
            wait_recv(yin.at[s, k], y_recv.at[s, k])
            zout[s, k] = part[s, k, y] + ((yin[s, k, 0] + yin[s, k, 1]) + yin[s, k, 2])
            if k:
                send(zout.at[s, k], zin.at[s, k - 1], z_send, z_recv.at[s], at(dz=k))

    def along_y(s, k):
        held = pre.at[s // 2, other_z[k], y, s % 2]
        for d in (2, 1, 3):
            send(held, held, gy_send, gy_recv.at[s // 2], at(dy=d))

    def over_z(s):
        wait_recv(zin.at[s], z_recv.at[s])
        total = zout[s, 0] + ((zin[s, 0] + zin[s, 1]) + zin[s, 2])
        pre[s // 2, z, y, s % 2] = total.astype(bf16)
        held = pre.at[s // 2, z, y, s % 2]
        for k in (3, 2, 1):
            send(held, held, gz_send, gz_recv.at[s, k - 1], at(dz=k))
        along_y(s, 0)

    def onward(s):
        for k in (1, 2, 3):
            wait_recv(pre.at[0, 0, 0, 0], gz_recv.at[s, k - 1])
            along_y(s, k)

    def project(f, e):
        if e:
            wait_recv(pre.at[f, pl.ds(0, Y - 1)], gy_recv.at[f])
            loads[4 + f].wait()
        first = c == 0
        to = (h + e) % H
        for i in range(X):
            rows = pl.ds(pl.multiple_of((to * X + i) * (C * SHARE), C * SHARE), C * SHARE)
            proj = None
            for k in range(Z):
                term = lax.dot_general(
                    pre[f, k].reshape(COLS, WIDE),
                    tok[f, rows, k * WIDE:(k + 1) * WIDE],
                    (((1,), (1,)), ((), ())),
                    preferred_element_type=f32,
                )
                proj = term if proj is None else proj + term
            low, high = proj[:, :SHARE], proj[:, SHARE:]
            own[f, e, i] = jnp.where(first, low, high)
            cout[f, e, i] = jnp.where(first, high, low).astype(bf16)
        send(cout.at[f, e], cin.at[f, e], c_send, c_recv.at[f, e], at(dc=1))

    def along_x(f, e):
        wait_recv(cin.at[f, e], c_recv.at[f, e])
        for d in (2, 1, 3):
            i = (x + d) % X
            xout[f, e, d - 1] = (own[f, e, i] + cin[f, e, i].astype(f32)).astype(bf16)
            send(
                xout.at[f, e, d - 1], xin.at[f, e, d - 1],
                x_send, x_recv.at[f, e], at(dx=d),
            )

    def over_x(f, e):
        total = own[f, e, x] + cin[f, e, x].astype(f32)
        wait_recv(xin.at[f, e], x_recv.at[f, e])
        for d in (1, 2, 3):
            total = total + xin[f, e, d - 1].astype(f32)
        return total

    def along_h(f):
        zhout[f] = over_x(f, 1).astype(bf16)
        send(zhout.at[f], zhin.at[f], h_send, h_recv.at[f], at(dh=1))

    terms(0, (0,))
    share(1)
    terms(1, (2,))
    share(3)
    over_y(0)
    over_y(1)
    over_z(0)
    over_y(2)
    over_z(1)
    onward(0)
    over_y(3)
    over_z(2)
    onward(1)
    over_z(3)
    onward(2)
    onward(3)
    project(0, 1)
    project(0, 0)
    wait_send(q.at[:, pl.ds(0, 2 * len(around) + 1)], a_send)
    wait_send(yin, y_send)
    wait_send(zin, z_send)
    project(1, 1)
    along_x(0, 1)
    project(1, 0)
    along_x(1, 1)
    along_x(0, 0)
    along_x(1, 0)
    along_h(0)
    wait_send(pre.at[:, pl.ds(0, Y - 1)], gy_send)
    wait_send(pre.at[pl.ds(0, 1), pl.ds(0, 3)].at[:, :, pl.ds(0, 2)], gz_send)
    along_h(1)
    wait_send(cout, c_send)
    proj = [over_x(f, 0) for f in (0, 1)]
    wait_send(xout, x_send)
    wait_send(zhout, h_send)
    for f in (0, 1):
        wait_recv(zhin.at[f], h_recv.at[f])
        proj[f] = proj[f] + zhin[f].astype(f32)
    out_ref[...] = jnp.sum((proj[0] * proj[1]).reshape(QUERIES, RANK, SHARE), axis=1)


def shards(*args):
    bf16, f32 = jnp.bfloat16, jnp.float32
    dma = pltpu.SemaphoreType.DMA
    return pl.pallas_call(
        kernel,
        out_shape=pltpu.VMEM((QUERIES, SHARE), f32),
        in_specs=[pl.BlockSpec(memory_space=pl.ANY)] * 6,
        out_specs=pl.BlockSpec(memory_space=pltpu.VMEM),
        scratch_shapes=[
            pltpu.VMEM((2, BLOCK, BLOCK), bf16),
            pltpu.VMEM((2, TOKENS, BLOCK), bf16),
            pltpu.VMEM((2, H * X * C, PIECE, COLS), bf16),
            pltpu.VMEM((4, Z, Y, ROWS, WIDE), f32),
            pltpu.VMEM((4, Z, Y - 1, ROWS, WIDE), f32),
            pltpu.VMEM((4, Z, ROWS, WIDE), f32),
            pltpu.VMEM((4, Z - 1, ROWS, WIDE), f32),
            pltpu.VMEM((2, Z, Y, 2, ROWS, WIDE), bf16),
            pltpu.VMEM((2, H, X, COLS, SHARE), f32),
            pltpu.VMEM((2, H, X, COLS, SHARE), bf16),
            pltpu.VMEM((2, H, X, COLS, SHARE), bf16),
            pltpu.VMEM((2, H, X - 1, COLS, SHARE), bf16),
            pltpu.VMEM((2, H, X - 1, COLS, SHARE), bf16),
            pltpu.VMEM((2, COLS, SHARE), bf16),
            pltpu.VMEM((2, COLS, SHARE), bf16),
            dma((6,)),
            dma, dma((2, 2)),
            dma, dma((4, Z)),
            dma, dma((4,)),
            dma, dma((4, Z - 1)),
            dma, dma((2,)),
            dma, dma((2, H)),
            dma, dma((2, H)),
            dma, dma((2,)),
        ],
        compiler_params=pltpu.CompilerParams(
            collective_id=0, has_side_effects=True, vmem_limit_bytes=60 << 20
        ),
    )(*args)


def solution(mesh):
    return jax.shard_map(
        shards,
        mesh=mesh,
        in_specs=(
            P("tok", "wid"),
            P("tok", "wid"),
            P(("tok", "wid"), None),
            P(("tok", "wid"), None),
            P("tok", "wid"),
            P("tok", "wid"),
        ),
        out_specs=P(None, ("tok", "wid")),
        check_vma=False,
    )
```

```python
import jax
import jax.numpy as jnp
from jax import lax
from jax.experimental import pallas as pl
from jax.experimental.pallas import tpu as pltpu
from jax.sharding import PartitionSpec as P

Y, Z, H, X, C = 4, 4, 2, 4, 2
QUERIES = 8
RANK = 16
COLS = QUERIES * RANK
BLOCK = 1024
TOKENS = 2048
PIECE = BLOCK // (H * X * C)
ROWS = COLS // Y // 2
WIDE = BLOCK // Z
SHARE = TOKENS // (H * X * C)


def kernel(
    g_hbm, a_hbm, qo_hbm, qi_hbm, og_hbm, ac_hbm,
    out_ref,
    inv, tok, q, part, yin, pin, two, zout, zin, pre, own, cout, cin, xout, xin, zhout, zhin,
    load_sem, a_send, a_recv, y_send, y_recv, p_send, p_recv, z_send, z_recv, gz_send, gz_recv,
    gy_send, gy_recv, c_send, c_recv, x_send, x_recv, h_send, h_recv,
):
    f32, bf16 = jnp.float32, jnp.bfloat16
    my_tok, my_wid = lax.axis_index("tok"), lax.axis_index("wid")
    y, z = my_tok // Z, my_tok % Z
    h, x, c = my_wid // (X * C), (my_wid // C) % X, my_wid % C

    other_z = (z, z + 1 - 2 * (z % 2), (z + 2) % Z, Z - 1 - z)

    def at(dy=0, dz=0, dh=0, dx=0, dc=0):
        return (
            (y + dy) % Y * Z + other_z[dz],
            (h + dh) % H * (X * C) + (x + dx) % X * C + (c + dc) % C,
        )

    def copy(src, dst, send_sem, recv_sem, peer):
        return pltpu.make_async_remote_copy(
            src_ref=src, dst_ref=dst, send_sem=send_sem, recv_sem=recv_sem,
            device_id=peer, device_id_type=pl.DeviceIdType.MESH,
        )

    def send(src, dst, send_sem, recv_sem, peer):
        copy(src, dst, send_sem, recv_sem, peer).start()

    def wait_recv(ref, sem):
        copy(ref, ref, load_sem.at[0], sem, at(dc=1)).wait_recv()

    def wait_send(ref, sem):
        copy(ref, ref, sem, load_sem.at[0], at(dc=1)).wait_send()

    loads = [
        pltpu.make_async_copy(src, dst, load_sem.at[i])
        for i, (src, dst) in enumerate((
            (qo_hbm, q.at[0, my_wid]),
            (qi_hbm, q.at[1, my_wid]),
            (g_hbm, inv.at[0]),
            (a_hbm, inv.at[1]),
            (og_hbm, tok.at[0]),
            (ac_hbm, tok.at[1]),
        ))
    ]
    for load in loads:
        load.start()

    around = [(d, e) for d in (2, 1, 3) for e in (0, 1)] + [(0, 1)]
    barrier = pltpu.get_barrier_semaphore()
    peers = (
        [at(dh=1)]
        + [at(dx=d, dc=e) for d, e in around]
        + [at(dy=d) for d in (2, 1, 3)]
        + [at(dz=d) for d in (1, 2, 3)]
    )
    for peer in peers:
        pl.semaphore_signal(barrier, inc=1, device_id=peer, device_id_type=pl.DeviceIdType.MESH)
    pl.semaphore_wait(barrier, len(peers))

    far = (my_wid + X * C) % (H * X * C)
    for f, src in enumerate((qo_hbm, qi_hbm)):
        send(src, q.at[f, my_wid], a_send, a_recv.at[f, 0], at(dh=1))
    for f, src in enumerate((qo_hbm, qi_hbm)):
        for d, e in around:
            send(src, q.at[f, my_wid], a_send, a_recv.at[f, 1], at(dx=d, dc=e))
    for f in (0, 1):
        wait_recv(q.at[f, far], a_recv.at[f, 0])
        for d, e in around:
            send(q.at[f, far], q.at[f, far], a_send, a_recv.at[f, 1], at(dx=d, dc=e))

    ORDER = (3, 2, 1, 0)
    PAIRED = (3,)

    def terms(f, first):
        loads[f].wait()
        loads[2 + f].wait()
        wait_recv(q.at[f, pl.ds(0, 2 * len(around))], a_recv.at[f, 1])
        query = q[f].reshape(BLOCK, COLS)
        for k in (ORDER if f == 0 else (3, 1, 2, 0)):
            wide = pl.ds(pl.multiple_of(other_z[k] * WIDE, WIDE), WIDE)
            term = lax.dot_general(
                query, inv[f, :, wide], (((0,), (0,)), ((), ())), preferred_element_type=f32
            ).reshape(Y, 2, ROWS, WIDE)
            part[2 * f, k] = term[:, 0]
            part[2 * f + 1, k] = term[:, 1]
            for s in first:
                share_out(s, k)
            if f == 1 and k == 1:
                for s in PAIRED:
                    for j in (1, 0):
                        send(
                            part.at[s, 2 * j + 1], pin.at[s - 2, j],
                            p_send.at[s - 2], p_recv.at[s - 2, j], at(dz=1),
                        )

    def share_out(s, k):
        for d in (2, 1, 3):
            send(
                part.at[s, k, (y + d) % Y], yin.at[s, k, d - 1],
                y_send.at[s], y_recv.at[s, k], at(dy=d),
            )

    def share(s):
        for k in ORDER:
            share_out(s, k)

    def pair(s):
        for k in (2, 0):
            j = k // 2
            wait_recv(pin.at[s - 2, j], p_recv.at[s - 2, j])
            two[s - 2, j] = part[s, k] + pin[s - 2, j]
            for d in (2, 1, 3):
                send(
                    two.at[s - 2, j, (y + d) % Y], yin.at[s, k, d - 1],
                    y_send.at[s], y_recv.at[s, k], at(dy=d),
                )

    def over_y(s):
        for k in ((2, 0) if s in PAIRED else ORDER):
            wait_recv(yin.at[s, k], y_recv.at[s, k])
            mine = two[s - 2, k // 2, y] if s in PAIRED else part[s, k, y]
            zout[s, k] = mine + ((yin[s, k, 0] + yin[s, k, 1]) + yin[s, k, 2])
            if k:
                send(
                    zout.at[s, k], zin.at[s, k - 1],
                    z_send.at[s], z_recv.at[s], at(dz=k),
                )

    def along_y(s, k):
        held = pre.at[s // 2, other_z[k], y, s % 2]
        for d in (2, 1, 3):
            send(held, held, gy_send, gy_recv.at[s // 2], at(dy=d))

    def over_z(s):
        if s not in PAIRED:
            wait_recv(zin.at[s], z_recv.at[s])
            total = zout[s, 0] + ((zin[s, 0] + zin[s, 1]) + zin[s, 2])
        else:
            wait_recv(zin.at[s, 1], z_recv.at[s])
            total = zout[s, 0] + zin[s, 1]
        pre[s // 2, z, y, s % 2] = total.astype(bf16)
        held = pre.at[s // 2, z, y, s % 2]
        for k in (3, 2, 1):
            send(held, held, gz_send, gz_recv.at[s, k - 1], at(dz=k))
        along_y(s, 0)

    def onward(s):
        for k in (1, 2, 3):
            wait_recv(pre.at[0, 0, 0, 0], gz_recv.at[s, k - 1])
            along_y(s, k)

    def project(f, e):
        if e:
            wait_recv(pre.at[f, pl.ds(0, Y - 1)], gy_recv.at[f])
            loads[4 + f].wait()
        first = c == 0
        to = (h + e) % H
        for i in range(X):
            rows = pl.ds(pl.multiple_of((to * X + i) * (C * SHARE), C * SHARE), C * SHARE)
            proj = None
            for k in range(Z):
                term = lax.dot_general(
                    pre[f, k].reshape(COLS, WIDE),
                    tok[f, rows, k * WIDE:(k + 1) * WIDE],
                    (((1,), (1,)), ((), ())),
                    preferred_element_type=f32,
                )
                proj = term if proj is None else proj + term
            low, high = proj[:, :SHARE], proj[:, SHARE:]
            own[f, e, i] = jnp.where(first, low, high)
            cout[f, e, i] = jnp.where(first, high, low).astype(bf16)
        send(cout.at[f, e], cin.at[f, e], c_send, c_recv.at[f, e], at(dc=1))

    def along_x(f, e):
        wait_recv(cin.at[f, e], c_recv.at[f, e])
        for d in (2, 1, 3):
            i = (x + d) % X
            xout[f, e, d - 1] = (own[f, e, i] + cin[f, e, i].astype(f32)).astype(bf16)
            send(
                xout.at[f, e, d - 1], xin.at[f, e, d - 1],
                x_send, x_recv.at[f, e], at(dx=d),
            )

    def over_x(f, e):
        total = own[f, e, x] + cin[f, e, x].astype(f32)
        wait_recv(xin.at[f, e], x_recv.at[f, e])
        for d in (1, 2, 3):
            total = total + xin[f, e, d - 1].astype(f32)
        return total

    def along_h(f):
        zhout[f] = over_x(f, 1).astype(bf16)
        send(zhout.at[f], zhin.at[f], h_send, h_recv.at[f], at(dh=1))

    terms(0, (0,))
    share(1)
    terms(1, (2,))
    over_y(0)
    pair(3)
    over_y(1)
    over_z(0)
    over_y(2)
    over_z(1)
    onward(0)
    over_y(3)
    over_z(2)
    onward(1)
    over_z(3)
    onward(2)
    onward(3)
    project(0, 1)
    project(0, 0)
    wait_send(q.at[:, pl.ds(0, 2 * len(around) + 1)], a_send)
    for s in range(4):
        if s in PAIRED:
            wait_send(pin.at[s - 2], p_send.at[s - 2])
            wait_send(yin.at[s, pl.ds(0, 2)], y_send.at[s])
            wait_send(zin.at[s, 1], z_send.at[s])
        else:
            wait_send(yin.at[s], y_send.at[s])
            wait_send(zin.at[s], z_send.at[s])
    along_x(0, 1)
    along_x(0, 0)
    project(1, 1)
    project(1, 0)
    along_x(1, 1)
    along_h(0)
    along_x(1, 0)
    wait_send(pre.at[:, pl.ds(0, Y - 1)], gy_send)
    wait_send(pre.at[pl.ds(0, 1), pl.ds(0, 3)].at[:, :, pl.ds(0, 2)], gz_send)
    along_h(1)
    wait_send(cout, c_send)
    proj = [over_x(f, 0) for f in (0, 1)]
    wait_send(xout, x_send)
    wait_send(zhout, h_send)
    for f in (0, 1):
        wait_recv(zhin.at[f], h_recv.at[f])
        proj[f] = proj[f] + zhin[f].astype(f32)
    out_ref[...] = jnp.sum((proj[0] * proj[1]).reshape(QUERIES, RANK, SHARE), axis=1)


def shards(*args):
    bf16, f32 = jnp.bfloat16, jnp.float32
    dma = pltpu.SemaphoreType.DMA
    return pl.pallas_call(
        kernel,
        out_shape=pltpu.VMEM((QUERIES, SHARE), f32),
        in_specs=[pl.BlockSpec(memory_space=pl.ANY)] * 6,
        out_specs=pl.BlockSpec(memory_space=pltpu.VMEM),
        scratch_shapes=[
            pltpu.VMEM((2, BLOCK, BLOCK), bf16),
            pltpu.VMEM((2, TOKENS, BLOCK), bf16),
            pltpu.VMEM((2, H * X * C, PIECE, COLS), bf16),
            pltpu.VMEM((4, Z, Y, ROWS, WIDE), f32),
            pltpu.VMEM((4, Z, Y - 1, ROWS, WIDE), f32),
            pltpu.VMEM((2, 2, Y, ROWS, WIDE), f32),
            pltpu.VMEM((2, 2, Y, ROWS, WIDE), f32),
            pltpu.VMEM((4, Z, ROWS, WIDE), f32),
            pltpu.VMEM((4, Z - 1, ROWS, WIDE), f32),
            pltpu.VMEM((2, Z, Y, 2, ROWS, WIDE), bf16),
            pltpu.VMEM((2, H, X, COLS, SHARE), f32),
            pltpu.VMEM((2, H, X, COLS, SHARE), bf16),
            pltpu.VMEM((2, H, X, COLS, SHARE), bf16),
            pltpu.VMEM((2, H, X - 1, COLS, SHARE), bf16),
            pltpu.VMEM((2, H, X - 1, COLS, SHARE), bf16),
            pltpu.VMEM((2, COLS, SHARE), bf16),
            pltpu.VMEM((2, COLS, SHARE), bf16),
            dma((6,)),
            dma, dma((2, 2)),
            dma((4,)), dma((4, Z)),
            dma((2,)), dma((2, 2)),
            dma((4,)), dma((4,)),
            dma, dma((4, Z - 1)),
            dma, dma((2,)),
            dma, dma((2, H)),
            dma, dma((2, H)),
            dma, dma((2,)),
        ],
        compiler_params=pltpu.CompilerParams(
            collective_id=0, has_side_effects=True, vmem_limit_bytes=60 << 20
        ),
    )(*args)


def solution(mesh):
    return jax.shard_map(
        shards,
        mesh=mesh,
        in_specs=(
            P("tok", "wid"),
            P("tok", "wid"),
            P(("tok", "wid"), None),
            P(("tok", "wid"), None),
            P("tok", "wid"),
            P("tok", "wid"),
        ),
        out_specs=P(None, ("tok", "wid")),
        check_vma=False,
    )
```

```python
import jax
import jax.numpy as jnp
from jax import lax
from jax.experimental import pallas as pl
from jax.experimental.pallas import tpu as pltpu
from jax.sharding import PartitionSpec as P

Y, Z, H, X, C = 4, 4, 2, 4, 2
QUERIES = 8
RANK = 16
COLS = QUERIES * RANK
BLOCK = 1024
TOKENS = 2048
PIECE = BLOCK // (H * X * C)
ROWS = COLS // Y // 2
WIDE = BLOCK // Z
SHARE = TOKENS // (H * X * C)


def kernel(
    g_hbm, a_hbm, qo_hbm, qi_hbm, og_hbm, ac_hbm,
    out_ref,
    inv, tok, q, part, yin, pin, two, zout, zin, pre, own, cout, cin, xout, xin, zhout, zhin,
    load_sem, a_send, a_recv, y_send, y_recv, p_send, p_recv, z_send, z_recv, gz_send, gz_recv,
    gy_send, gy_recv, c_send, c_recv, x_send, x_recv, h_send, h_recv,
):
    f32, bf16 = jnp.float32, jnp.bfloat16
    my_tok, my_wid = lax.axis_index("tok"), lax.axis_index("wid")
    y, z = my_tok // Z, my_tok % Z
    h, x, c = my_wid // (X * C), (my_wid // C) % X, my_wid % C

    other_z = (z, z + 1 - 2 * (z % 2), (z + 2) % Z, Z - 1 - z)

    def at(dy=0, dz=0, dh=0, dx=0, dc=0):
        return (
            (y + dy) % Y * Z + other_z[dz],
            (h + dh) % H * (X * C) + (x + dx) % X * C + (c + dc) % C,
        )

    def copy(src, dst, send_sem, recv_sem, peer):
        return pltpu.make_async_remote_copy(
            src_ref=src, dst_ref=dst, send_sem=send_sem, recv_sem=recv_sem,
            device_id=peer, device_id_type=pl.DeviceIdType.MESH,
        )

    def send(src, dst, send_sem, recv_sem, peer):
        copy(src, dst, send_sem, recv_sem, peer).start()

    def wait_recv(ref, sem):
        copy(ref, ref, load_sem.at[0], sem, at(dc=1)).wait_recv()

    def wait_send(ref, sem):
        copy(ref, ref, sem, load_sem.at[0], at(dc=1)).wait_send()

    loads = [
        pltpu.make_async_copy(src, dst, load_sem.at[i])
        for i, (src, dst) in enumerate((
            (qo_hbm, q.at[0, my_wid]),
            (qi_hbm, q.at[1, my_wid]),
            (g_hbm, inv.at[0]),
            (a_hbm, inv.at[1]),
            (og_hbm, tok.at[0]),
            (ac_hbm, tok.at[1]),
        ))
    ]
    around = [(d, e) for d in (2, 1, 3) for e in (0, 1)] + [(0, 1)]
    barrier = pltpu.get_barrier_semaphore()
    peers = (
        [at(dh=1)]
        + [at(dx=d, dc=e) for d, e in around]
        + [at(dy=d) for d in (2, 1, 3)]
        + [at(dz=d) for d in (1, 2, 3)]
    )
    for peer in peers:
        pl.semaphore_signal(barrier, inc=1, device_id=peer, device_id_type=pl.DeviceIdType.MESH)
    for load in loads:
        load.start()
    pl.semaphore_wait(barrier, len(peers))

    far = (my_wid + X * C) % (H * X * C)
    for f, src in enumerate((qo_hbm, qi_hbm)):
        send(src, q.at[f, my_wid], a_send, a_recv.at[f, 0], at(dh=1))
    for f, src in enumerate((qo_hbm, qi_hbm)):
        for d, e in around:
            send(src, q.at[f, my_wid], a_send, a_recv.at[f, 1], at(dx=d, dc=e))
    for f in (0, 1):
        wait_recv(q.at[f, far], a_recv.at[f, 0])
        for d, e in around:
            send(q.at[f, far], q.at[f, far], a_send, a_recv.at[f, 1], at(dx=d, dc=e))

    ORDER = (3, 2, 1, 0)
    PAIRED = (3,)

    def terms(f, first):
        loads[f].wait()
        loads[2 + f].wait()
        wait_recv(q.at[f, pl.ds(0, 2 * len(around))], a_recv.at[f, 1])
        query = q[f].reshape(BLOCK, COLS)
        for k in (ORDER if f == 0 else (3, 1, 2, 0)):
            wide = pl.ds(pl.multiple_of(other_z[k] * WIDE, WIDE), WIDE)
            term = lax.dot_general(
                query, inv[f, :, wide], (((0,), (0,)), ((), ())), preferred_element_type=f32
            ).reshape(Y, 2, ROWS, WIDE)
            part[2 * f, k] = term[:, 0]
            part[2 * f + 1, k] = term[:, 1]
            for s in first:
                share_out(s, k)
            if f == 1 and k == 1:
                for s in PAIRED:
                    for j in (1, 0):
                        send(
                            part.at[s, 2 * j + 1], pin.at[s - 2, j],
                            p_send.at[s - 2], p_recv.at[s - 2, j], at(dz=1),
                        )

    def share_out(s, k):
        for d in (2, 1, 3):
            send(
                part.at[s, k, (y + d) % Y], yin.at[s, k, d - 1],
                y_send.at[s], y_recv.at[s, k], at(dy=d),
            )

    def share(s):
        for k in ORDER:
            share_out(s, k)

    def pair(s):
        for k in (2, 0):
            j = k // 2
            wait_recv(pin.at[s - 2, j], p_recv.at[s - 2, j])
            two[s - 2, j] = part[s, k] + pin[s - 2, j]
            for d in (2, 1, 3):
                send(
                    two.at[s - 2, j, (y + d) % Y], yin.at[s, k, d - 1],
                    y_send.at[s], y_recv.at[s, k], at(dy=d),
                )

    def over_y(s):
        for k in ((2, 0) if s in PAIRED else ORDER):
            wait_recv(yin.at[s, k], y_recv.at[s, k])
            mine = two[s - 2, k // 2, y] if s in PAIRED else part[s, k, y]
            zout[s, k] = mine + ((yin[s, k, 0] + yin[s, k, 1]) + yin[s, k, 2])
            if k:
                send(
                    zout.at[s, k], zin.at[s, k - 1],
                    z_send.at[s], z_recv.at[s], at(dz=k),
                )

    def along_y(s, k):
        held = pre.at[s // 2, other_z[k], y, s % 2]
        for d in (2, 1, 3):
            send(held, held, gy_send, gy_recv.at[s // 2], at(dy=d))

    def over_z(s):
        if s not in PAIRED:
            wait_recv(zin.at[s], z_recv.at[s])
            total = zout[s, 0] + ((zin[s, 0] + zin[s, 1]) + zin[s, 2])
        else:
            wait_recv(zin.at[s, 1], z_recv.at[s])
            total = zout[s, 0] + zin[s, 1]
        pre[s // 2, z, y, s % 2] = total.astype(bf16)
        held = pre.at[s // 2, z, y, s % 2]
        for k in (3, 2, 1):
            send(held, held, gz_send, gz_recv.at[s, k - 1], at(dz=k))
        along_y(s, 0)

    def onward(s):
        for k in (1, 2, 3):
            wait_recv(pre.at[0, 0, 0, 0], gz_recv.at[s, k - 1])
            along_y(s, k)

    def project(f, e):
        if e:
            wait_recv(pre.at[f, pl.ds(0, Y - 1)], gy_recv.at[f])
            loads[4 + f].wait()
        first = c == 0
        to = (h + e) % H
        for i in range(X):
            rows = pl.ds(pl.multiple_of((to * X + i) * (C * SHARE), C * SHARE), C * SHARE)
            proj = None
            for k in range(Z):
                term = lax.dot_general(
                    pre[f, k].reshape(COLS, WIDE),
                    tok[f, rows, k * WIDE:(k + 1) * WIDE],
                    (((1,), (1,)), ((), ())),
                    preferred_element_type=f32,
                )
                proj = term if proj is None else proj + term
            low, high = proj[:, :SHARE], proj[:, SHARE:]
            own[f, e, i] = jnp.where(first, low, high)
            cout[f, e, i] = jnp.where(first, high, low).astype(bf16)
        send(cout.at[f, e], cin.at[f, e], c_send, c_recv.at[f, e], at(dc=1))

    def along_x(f, e):
        wait_recv(cin.at[f, e], c_recv.at[f, e])
        for d in (2, 1, 3):
            i = (x + d) % X
            xout[f, e, d - 1] = (own[f, e, i] + cin[f, e, i].astype(f32)).astype(bf16)
            send(
                xout.at[f, e, d - 1], xin.at[f, e, d - 1],
                x_send, x_recv.at[f, e], at(dx=d),
            )

    def over_x(f, e):
        total = own[f, e, x] + cin[f, e, x].astype(f32)
        wait_recv(xin.at[f, e], x_recv.at[f, e])
        for d in (1, 2, 3):
            total = total + xin[f, e, d - 1].astype(f32)
        return total

    def along_h(f):
        zhout[f] = over_x(f, 1).astype(bf16)
        send(zhout.at[f], zhin.at[f], h_send, h_recv.at[f], at(dh=1))

    terms(0, (0,))
    share(1)
    terms(1, (2,))
    over_y(0)
    pair(3)
    over_y(1)
    over_z(0)
    over_y(2)
    over_z(1)
    onward(0)
    over_y(3)
    over_z(2)
    onward(1)
    over_z(3)
    onward(2)
    onward(3)
    project(0, 1)
    project(0, 0)
    wait_send(q.at[:, pl.ds(0, 2 * len(around) + 1)], a_send)
    for s in range(4):
        if s in PAIRED:
            wait_send(pin.at[s - 2], p_send.at[s - 2])
            wait_send(yin.at[s, pl.ds(0, 2)], y_send.at[s])
            wait_send(zin.at[s, 1], z_send.at[s])
        else:
            wait_send(yin.at[s], y_send.at[s])
            wait_send(zin.at[s], z_send.at[s])
    along_x(0, 1)
    along_x(0, 0)
    project(1, 1)
    project(1, 0)
    along_x(1, 1)
    along_h(0)
    along_x(1, 0)
    wait_send(pre.at[:, pl.ds(0, Y - 1)], gy_send)
    wait_send(pre.at[pl.ds(0, 1), pl.ds(0, 3)].at[:, :, pl.ds(0, 2)], gz_send)
    along_h(1)
    wait_send(cout, c_send)
    proj = [over_x(f, 0) for f in (0, 1)]
    wait_send(xout, x_send)
    wait_send(zhout, h_send)
    for f in (0, 1):
        wait_recv(zhin.at[f], h_recv.at[f])
        proj[f] = proj[f] + zhin[f].astype(f32)
    out_ref[...] = jnp.sum((proj[0] * proj[1]).reshape(QUERIES, RANK, SHARE), axis=1)


def shards(*args):
    bf16, f32 = jnp.bfloat16, jnp.float32
    dma = pltpu.SemaphoreType.DMA
    return pl.pallas_call(
        kernel,
        out_shape=pltpu.VMEM((QUERIES, SHARE), f32),
        in_specs=[pl.BlockSpec(memory_space=pl.ANY)] * 6,
        out_specs=pl.BlockSpec(memory_space=pltpu.VMEM),
        scratch_shapes=[
            pltpu.VMEM((2, BLOCK, BLOCK), bf16),
            pltpu.VMEM((2, TOKENS, BLOCK), bf16),
            pltpu.VMEM((2, H * X * C, PIECE, COLS), bf16),
            pltpu.VMEM((4, Z, Y, ROWS, WIDE), f32),
            pltpu.VMEM((4, Z, Y - 1, ROWS, WIDE), f32),
            pltpu.VMEM((2, 2, Y, ROWS, WIDE), f32),
            pltpu.VMEM((2, 2, Y, ROWS, WIDE), f32),
            pltpu.VMEM((4, Z, ROWS, WIDE), f32),
            pltpu.VMEM((4, Z - 1, ROWS, WIDE), f32),
            pltpu.VMEM((2, Z, Y, 2, ROWS, WIDE), bf16),
            pltpu.VMEM((2, H, X, COLS, SHARE), f32),
            pltpu.VMEM((2, H, X, COLS, SHARE), bf16),
            pltpu.VMEM((2, H, X, COLS, SHARE), bf16),
            pltpu.VMEM((2, H, X - 1, COLS, SHARE), bf16),
            pltpu.VMEM((2, H, X - 1, COLS, SHARE), bf16),
            pltpu.VMEM((2, COLS, SHARE), bf16),
            pltpu.VMEM((2, COLS, SHARE), bf16),
            dma((6,)),
            dma, dma((2, 2)),
            dma((4,)), dma((4, Z)),
            dma((2,)), dma((2, 2)),
            dma((4,)), dma((4,)),
            dma, dma((4, Z - 1)),
            dma, dma((2,)),
            dma, dma((2, H)),
            dma, dma((2, H)),
            dma, dma((2,)),
        ],
        compiler_params=pltpu.CompilerParams(
            collective_id=0, has_side_effects=True, vmem_limit_bytes=60 << 20
        ),
    )(*args)


def solution(mesh):
    return jax.shard_map(
        shards,
        mesh=mesh,
        in_specs=(
            P("tok", "wid"),
            P("tok", "wid"),
            P(("tok", "wid"), None),
            P(("tok", "wid"), None),
            P("tok", "wid"),
            P("tok", "wid"),
        ),
        out_specs=P(None, ("tok", "wid")),
        check_vma=False,
    )
```
